32 devices in a mesh: dp: 8 (over z, y), fsdp: 4 (over x, core).
Axes of the slice: x: 2, y: 2, z: 4, core: 2. Of those that a mesh axis runs over, the one named last changes fastest.
Arguments:
- tokens: bfloat16 [65536, 768], P(('dp', 'fsdp')), may hold values from -6 to 6
- cotangent: bfloat16 [65536, 768], P(('dp', 'fsdp')), may hold values from -6 to 6
- bucket_code: int32 [64], P(('dp', 'fsdp')), may hold values from 0 to 2, as said below
- qkv_weight: bfloat16 [768, 2304], P(('dp', 'fsdp')), may hold values from -0.21875 to 0.21875
- qkv_bias: bfloat16 [2304], P(('dp', 'fsdp')), may hold values from -1.75 to 1.75
- projection: bfloat16 [256, 1024], P(('dp', 'fsdp')), may hold values from -0.1875 to 0.1875
- out_weight: bfloat16 [768, 768], P(('dp', 'fsdp')), may hold values from -2.5 to 2.5
- out_bias: bfloat16 [768], P(('dp', 'fsdp')), may hold values from -1.75 to 1.75
- norm_gain: bfloat16 [768], P(('dp', 'fsdp')), may hold values from 0.5 to 1.5
- norm_shift: bfloat16 [768], P(('dp', 'fsdp')), may hold values from -1.75 to 1.75
- up_weight: bfloat16 [768, 3072], P(('dp', 'fsdp')), may hold values from -0.21875 to 0.21875
- up_bias: bfloat16 [3072], P(('dp', 'fsdp')), may hold values from -3 to 3
- down_weight: bfloat16 [3072, 768], P(('dp', 'fsdp')), may hold values from -0.109375 to 0.109375
- down_bias: bfloat16 [768], P(('dp', 'fsdp')), may hold values from -1.75 to 1.75
- final_gain: bfloat16 [768], P(('dp', 'fsdp')), may hold values from 0.5 to 1.5
- final_shift: bfloat16 [768], P(('dp', 'fsdp')), may hold values from -1.75 to 1.75
Outputs:
- layer_output: bfloat16 [65536, 768], P(('dp', 'fsdp'))
- token_grad: bfloat16 [65536, 768], P(('dp', 'fsdp'))
- grad_qkv_weight: float32 [768, 2304], P(('dp', 'fsdp'))
- grad_qkv_bias: float32 [2304], P(('dp', 'fsdp'))
- grad_projection: float32 [256, 1024], P(('dp', 'fsdp'))
- grad_out_weight: float32 [768, 768], P(('dp', 'fsdp'))
- grad_out_bias: float32 [768], P(('dp', 'fsdp'))
- grad_norm_gain: float32 [768], P(('dp', 'fsdp'))
- grad_norm_shift: float32 [768], P(('dp', 'fsdp'))
- grad_up_weight: float32 [768, 3072], P(('dp', 'fsdp'))
- grad_up_bias: float32 [3072], P(('dp', 'fsdp'))
- grad_down_weight: float32 [3072, 768], P(('dp', 'fsdp'))
- grad_down_bias: float32 [768], P(('dp', 'fsdp'))
- grad_final_gain: float32 [768], P(('dp', 'fsdp'))
- grad_final_shift: float32 [768], P(('dp', 'fsdp'))
The draws below stay inside these ranges and needn't reach their ends.
Inputs may be any that keep to these rules, and one draw needn't show every extreme that they name: bucket_code of a buffer tells whether it holds one sequence of 1024 tokens (0), one of 512 tokens (1) or two of 512 tokens (2); all three occur.
All inputs are finite; a program needn't handle non-finite values.
Results may differ from the reference program's by a relative error of at most 0.015.
Values may be sent and summed in bfloat16 or wider, within the bound.
No kernel may reach another device: no remote copies, remote signals or barrier semaphores. Data moves between devices by JAX's collectives and lax.ppermute only.
A program may use at most 320 MiB of HBM per device.

```python
import math
import jax
import jax.numpy as jnp
from jax import lax

D = 768
HEADS = 12
HDIM = 64
FF = 3072
K = 256
SHORT = 512
LONG = 1024
TOKENS = 65536
BUFFERS = 64


def draw_bucket_code(key, part):
    bucket_values = jax.random.randint(key, (BUFFERS,), 0, 3).astype(jnp.int32)
    return bucket_values.at[0].set(0).at[1].set(2).at[2].set(1)


def raised(drawn, own_key, source, target, blocks, factor):
    owner, partner = [(jnp.arange(drawn.shape[dim]) // (drawn.shape[dim] // blocks)).reshape([-1 if axis == dim else 1 for axis in range(drawn.ndim)]) for dim in (source, target)]
    chosen = jax.random.permutation(own_key, blocks)[partner]
    strong = (owner == chosen) | (owner == (partner + blocks // 2) % blocks)
    return jnp.where(strong, factor * drawn, drawn)


def shard_levels(own_key, dims, cuts, smallest, top_value):
    level, own = 1.0, jax.random.fold_in(own_key, 6)
    for position, parts in cuts:
        heights = jnp.exp(jax.random.uniform(jax.random.fold_in(own, position), (parts,), jnp.float32, smallest / len(cuts), top_value / len(cuts)))
        level = level * jnp.repeat(heights, dims[position] // parts).reshape([-1 if axis == position else 1 for axis in range(len(dims))])
    return level


def centred(key, extent, width, reach, shards=(), kind=jnp.bfloat16):
    loudness = shard_levels(key, extent, shards, -0.22, 0.18) if shards else 1.0
    values = jax.random.normal(key, extent, jnp.float32) * width * loudness
    return jnp.minimum(jnp.maximum(values, -reach), reach).astype(kind)


def bell_draw_with(rng, shape, width, limit, split, heavy, dtype=jnp.bfloat16):
    drawn = width * jax.random.normal(rng, shape, jnp.float32)
    if split:
        drawn = drawn * shard_levels(rng, shape, split, -0.22, 0.18)
    return jnp.clip(raised(drawn, jax.random.fold_in(rng, 3), *heavy), -limit, limit).astype(dtype)


def setup_inputs(seed: int = 0) -> dict:
    streams_of = jax.random.split(jax.random.key(seed), 17)
    return {
        "tokens": centred(streams_of[0], (TOKENS, D), 1.0, 6.0, ((0, 32),)),
        "cotangent": bell_draw_with(streams_of[1], (TOKENS, D), 1.0, 6.0, ((0, 32),), (0, 1, 32, 2.75)),
        "bucket_code": draw_bucket_code(jax.random.fold_in(streams_of[16], 71), 0),
        "qkv_weight": centred(streams_of[3], (D, 3 * D), D ** -0.5, 0.21875, ((0, 32),)),
        "qkv_bias": centred(streams_of[4], (3 * D,), 0.3, 1.75, ((0, 32),)),
        "projection": centred(streams_of[5], (K, LONG), LONG ** -0.5, 0.1875, ((0, 32),)),
        "out_weight": centred(streams_of[6], (D, D), (D // 128) ** -0.5, 2.5, ((0, 32),)),
        "out_bias": centred(streams_of[7], (D,), 0.3, 1.75, ((0, 32),)),
        "norm_gain": jnp.clip(1.0 + 0.1 * jax.random.normal(streams_of[8], (D,), jnp.float32), 0.5, 1.5).astype(jnp.bfloat16),
        "norm_shift": centred(streams_of[9], (D,), 0.3, 1.75, ((0, 32),)),
        "up_weight": centred(streams_of[10], (D, FF), D ** -0.5, 0.21875, ((0, 32),)),
        "up_bias": centred(streams_of[11], (FF,), 0.5, 3.0, ((0, 32),)),
        "down_weight": centred(streams_of[12], (FF, D), FF ** -0.5, 0.109375, ((0, 32),)),
        "down_bias": centred(streams_of[13], (D,), 0.3, 1.75, ((0, 32),)),
        "final_gain": jnp.clip(1.0 + 0.1 * jax.random.normal(streams_of[14], (D,), jnp.float32), 0.5, 1.5).astype(jnp.bfloat16),
        "final_shift": centred(streams_of[15], (D,), 0.3, 1.75, ((0, 32),)),
    }


EPSILON = 1e-05

@jax.custom_vjp
def low(v):
    return lax.optimization_barrier(v.astype(jnp.bfloat16)).astype(jnp.float32)

@jax.custom_vjp
def low_back(v):
    return v

def low_keep(v):
    return (low(v), None)

def low_pass(kept, grad):
    return (grad,)

def back_keep(v):
    return (v, None)

def back_low(kept, grad):
    return (low(grad),)
low.defvjp(low_keep, low_pass)
low_back.defvjp(back_keep, back_low)

def product(former, latter):
    return jnp.dot(former, latter, precision=lax.Precision.HIGHEST)

def normalize(hidden, gain, shift):
    center = hidden - lax.optimization_barrier(jnp.mean(hidden, -1, keepdims=True))
    spread = lax.optimization_barrier(jnp.mean(center * center, -1, keepdims=True))
    return center * lax.rsqrt(spread + EPSILON) * gain + shift

def split_heads(matrix):
    return matrix.reshape(matrix.shape[0], HEADS, HDIM)

def attend(queries, key_proj, value_proj):
    score_scale = 1.0 / math.sqrt(HDIM)
    scores = jnp.einsum('qhd,khd->hqk', split_heads(queries), split_heads(key_proj), precision=lax.Precision.HIGHEST)
    scores = low_back(scores * score_scale)
    highest = lax.optimization_barrier(jnp.max(scores, -1, keepdims=True))
    weights = jnp.exp(scores - highest)
    probabilities = low(weights / lax.optimization_barrier(jnp.sum(weights, -1, keepdims=True)))
    context = jnp.einsum('hqk,khd->qhd', probabilities, split_heads(value_proj), precision=lax.Precision.HIGHEST)
    return context.reshape(queries.shape[0], D)

def layer_buffer(params, block_tokens, bucket):
    qkv_weight, qkv_bias, projection, out_weight, out_bias, norm_gain, norm_shift, up_weight, up_bias, down_weight, down_bias, final_gain, final_shift = params
    half_rows = SHORT
    single = bucket == 0
    joined = low_back(low(product(block_tokens, qkv_weight) + qkv_bias))
    first_block = projection[:, :half_rows]
    second_block = jnp.where(single, projection[:, half_rows:], first_block)
    lower = product(first_block, joined[:half_rows, D:])
    upper = product(second_block, joined[half_rows:, D:])
    rounded_merged = low_back(low(lower + upper))
    rounded_lower = low_back(low(lower))
    rounded_upper = low_back(low(upper))
    proj_first = jnp.where(single, rounded_merged, rounded_lower)
    proj_second = jnp.where(single, rounded_merged, rounded_upper)
    queries = joined[:, :D]
    context_first = attend(queries[:half_rows], proj_first[:, :D], proj_first[:, D:])
    context_second = attend(queries[half_rows:], proj_second[:, :D], proj_second[:, D:])
    context = low_back(low(jnp.concatenate([context_first, context_second], 0)))
    attended = low_back(product(context, out_weight) + out_bias)
    hidden_one = block_tokens + attended
    normed = low(normalize(hidden_one, norm_gain, norm_shift))
    upward = low_back(product(normed, up_weight) + up_bias)
    active = low(jax.nn.gelu(upward, approximate=False))
    downward = low_back(product(active, down_weight) + down_bias)
    return normalize(normed + downward, final_gain, final_shift)

def reference(tokens, cotangent, bucket_code, qkv_weight, qkv_bias, projection, out_weight, out_bias, norm_gain, norm_shift, up_weight, up_bias, down_weight, down_bias, final_gain, final_shift):
    params = tuple((weight.astype(jnp.float32) for weight in (qkv_weight, qkv_bias, projection, out_weight, out_bias, norm_gain, norm_shift, up_weight, up_bias, down_weight, down_bias, final_gain, final_shift)))
    buffer_count = bucket_code.shape[0]
    stacked = tokens.astype(jnp.float32).reshape(buffer_count, LONG, D)
    positions = lax.broadcasted_iota(jnp.int32, (1, LONG, 1), 1)
    live_rows = jnp.where((bucket_code[:, None, None] == 1) & (positions >= SHORT), 0.0, 1.0).astype(jnp.float32)

    def forward(weights, inputs):

        def advance(running, element):
            block_tokens, bucket = element
            return (running, jax.checkpoint(layer_buffer)(weights, block_tokens, bucket))
        _, outcome = lax.scan(advance, jnp.zeros((), jnp.float32), (inputs, bucket_code))
        return outcome
    result, pullback = jax.vjp(forward, params, stacked)
    gradients, grad_tokens = pullback(cotangent.astype(jnp.float32).reshape(buffer_count, LONG, D) * live_rows)
    layer_output = (result * live_rows).reshape(-1, D).astype(jnp.bfloat16)
    token_grad = grad_tokens.reshape(-1, D).astype(jnp.bfloat16)
    return (layer_output, token_grad, gradients[0], gradients[1], gradients[2], gradients[3], gradients[4], gradients[5], gradients[6], gradients[7], gradients[8], gradients[9], gradients[10], gradients[11], gradients[12])
```

```python
import functools
import math
import jax, jax.numpy as jnp
from jax import lax
from jax.experimental import pallas as pl
from jax.experimental.pallas import tpu as pltpu
from jax.sharding import PartitionSpec as P

HEADS = 12
EPS = 1e-5
BF = jnp.bfloat16
F32 = jnp.float32
NT = (((1,), (1,)), ((), ()))
TN = (((0,), (0,)), ((), ()))
VMEM_LIMIT = 60 * 1024 * 1024


def mm(a, b):
    return jnp.dot(a, b, preferred_element_type=F32)


def mm_nt(a, b):
    return lax.dot_general(a, b, NT, preferred_element_type=F32)


def mm_tn(a, b):
    return lax.dot_general(a, b, TN, preferred_element_type=F32)


def params(n=1):
    return pltpu.CompilerParams(dimension_semantics=("arbitrary",) * n, vmem_limit_bytes=VMEM_LIMIT)


def whole(shape):
    return pl.BlockSpec(shape, lambda i, *_: (0,) * len(shape), pipeline_mode=pl.Buffered(1))


def qkv_body(code, x_ref, w_ref, b_ref, p_ref, q_ref, kv_ref, pk_ref, low):
    step = pl.program_id(0)
    upper = step % 2
    single = code[step // 2] == 0
    half = x_ref.shape[0]
    d = x_ref.shape[1]
    x = x_ref[...]
    q_ref[...] = (mm(x, w_ref[:, :d]) + b_ref[:, :d]).astype(BF)
    for j in (1, 2):
        kv_ref[:, (j - 1) * d : j * d] = (
            mm(x, w_ref[:, j * d : (j + 1) * d]) + b_ref[:, j * d : (j + 1) * d]
        ).astype(BF)
    second = jnp.logical_and(upper == 1, single)
    block = jnp.where(second, p_ref[:, half:], p_ref[:, :half])
    made = mm(block, kv_ref[...])

    @pl.when(upper == 0)
    def _():
        low[...] = made

    @pl.when(upper == 1)
    def _():
        merged = low[...] + made
        pk_ref[0] = jnp.where(single, merged, low[...]).astype(BF)
        pk_ref[1] = jnp.where(single, merged, made).astype(BF)


def qkv_call(code, x, w, b, proj):
    n, d = x.shape
    k = proj.shape[0]
    half = proj.shape[1] // 2
    steps = n // half
    return pl.pallas_call(
        qkv_body,
        grid_spec=pltpu.PrefetchScalarGridSpec(
            num_scalar_prefetch=1,
            grid=(steps,),
            in_specs=[
                pl.BlockSpec((half, d), lambda i, c: (i, 0)),
                whole(w.shape),
                whole(b.shape),
                whole(proj.shape),
            ],
            out_specs=[
                pl.BlockSpec((half, d), lambda i, c: (i, 0)),
                pl.BlockSpec((half, 2 * d), lambda i, c: (i, 0)),
                pl.BlockSpec((2, k, 2 * d), lambda i, c: (i // 2, 0, 0)),
            ],
            scratch_shapes=[pltpu.VMEM((k, 2 * d), F32)],
        ),
        out_shape=[
            jax.ShapeDtypeStruct((n, d), BF),
            jax.ShapeDtypeStruct((n, 2 * d), BF),
            jax.ShapeDtypeStruct((steps, k, 2 * d), BF),
        ],
        compiler_params=params(),
        name="qkv",
    )(code, x, w, b, proj)


def row_norm(h):
    mean = jnp.mean(h, -1, keepdims=True)
    c = h - mean
    r = lax.rsqrt(jnp.mean(c * c, -1, keepdims=True) + EPS)
    return c * r, r


def pair_mask(rows):
    lane = lax.broadcasted_iota(jnp.int32, (rows, 128), 1)
    return lane < 64


def attend_body(natural, x_ref, q_ref, pk_ref, w_ref, v_ref, p_ref, c_ref, h_ref, n_ref):
    d = q_ref.shape[1]
    k = pk_ref.shape[1]
    scale = 1.0 / math.sqrt(d // HEADS)
    left = pair_mask(k)
    for i in range(HEADS // 2):
        cols = slice(128 * i, 128 * (i + 1))
        vcols = slice(d + 128 * i, d + 128 * (i + 1))
        q = q_ref[:, cols]
        kp = pk_ref[0, :, cols] * jnp.asarray(scale, BF)
        vp = pk_ref[0, :, vcols]
        zero = jnp.zeros_like(kp)
        total = None
        for s in range(2):
            keep = left if s == 0 else jnp.logical_not(left)
            km = jnp.where(keep, kp, zero)
            vm = jnp.where(keep, vp, zero)
            sc = mm_nt(km, q)
            e = jnp.exp(sc - jnp.max(sc, 0, keepdims=True))
            p = (e * (1.0 / jnp.sum(e, 0, keepdims=True))).astype(BF)
            p_ref[0, 2 * i + s] = p
            part = mm_tn(p, vm)
            total = part if total is None else total + part
        c_ref[:, cols] = total.astype(BF)
    h = x_ref[...].astype(F32) + mm(c_ref[...], w_ref[...]) + v_ref[0:1, :]
    h_ref[...] = h
    xhat, _ = row_norm(h)
    n_ref[...] = (xhat * v_ref[1:2, :] + v_ref[2:3, :]).astype(BF)


def attend_call(x, q, pk, w, vec):
    n, d = x.shape
    steps, k, _ = pk.shape
    half = n // steps
    row = pl.BlockSpec((half, d), lambda i: (i, 0))
    return pl.pallas_call(
        lambda *refs: attend_body(True, *refs),
        grid=(steps,),
        in_specs=[
            row,
            row,
            pl.BlockSpec((1, k, 2 * d), lambda i: (i, 0, 0)),
            whole(w.shape),
            whole(vec.shape),
        ],
        out_specs=[
            pl.BlockSpec((1, HEADS, k, half), lambda i: (i, 0, 0, 0)),
            row,
            row,
            row,
        ],
        out_shape=[
            jax.ShapeDtypeStruct((steps, HEADS, k, half), BF),
            jax.ShapeDtypeStruct((n, d), BF),
            jax.ShapeDtypeStruct((n, d), F32),
            jax.ShapeDtypeStruct((n, d), BF),
        ],
        compiler_params=params(),
        name="attend",
    )(x, q, pk, w, vec)


def gelu_parts(u):
    e = jnp.exp(-0.5 * u * u)
    a = jnp.abs(u)
    t = 1.0 / (1.0 + (0.3275911 * 0.7071067811865476) * a)
    poly = t * (0.254829592 + t * (-0.284496736 + t * (1.421413741 + t * (-1.453152027 + t * 1.061405429))))
    tail = 0.5 * poly * e
    phi = jnp.where(u < 0, tail, 1.0 - tail)
    return u * phi, phi + u * (e * 0.3989422804014327)


def forward_body(code, n_ref, cot_ref, wu_ref, bu_ref, wd_ref, v_ref, a_ref, g_ref, o_ref, gh_ref, gd_ref, s_ref):
    step = pl.program_id(0)
    steps = pl.num_programs(0)
    per = steps // code.shape[0]
    half_steps = per // 2
    dead = jnp.logical_and(code[step // per] == 1, step % per >= half_steps)
    live = jnp.where(dead, 0.0, 1.0).astype(F32)
    d = n_ref.shape[1]
    n = n_ref[...]
    h = n.astype(F32) + v_ref[0:1, :]
    for j in range(wu_ref.shape[1] // d):
        cols = slice(j * d, (j + 1) * d)
        u = mm(n, wu_ref[:, cols]) + bu_ref[:, cols]
        act, slope = gelu_parts(u)
        act = act.astype(BF)
        a_ref[:, cols] = act
        g_ref[:, cols] = slope.astype(BF)
        h = h + mm(act, wd_ref[cols, :])
    xhat, r = row_norm(h)
    o_ref[...] = (live * (xhat * v_ref[1:2, :] + v_ref[2:3, :])).astype(BF)
    gf = cot_ref[...].astype(F32) * live
    g = gf * v_ref[1:2, :]
    gx = gf * xhat
    gh = r * (g - jnp.mean(g, -1, keepdims=True) - xhat * jnp.mean(g * xhat, -1, keepdims=True))
    gh_ref[...] = gh
    gd = gh.astype(BF)
    gd_ref[...] = gd

    @pl.when(step == 0)
    def _():
        s_ref[...] = jnp.zeros_like(s_ref)

    s_ref[0:1, :] += jnp.sum(gx, 0, keepdims=True)
    s_ref[1:2, :] += jnp.sum(gf, 0, keepdims=True)
    s_ref[2:3, :] += jnp.sum(gd.astype(F32), 0, keepdims=True)


def forward_call(code, n, cot, wu, bu, wd, vec, tile=512):
    rows, d = n.shape
    ff = wu.shape[1]
    row = pl.BlockSpec((tile, d), lambda i, c: (i, 0))
    wide = pl.BlockSpec((tile, ff), lambda i, c: (i, 0))
    return pl.pallas_call(
        forward_body,
        grid_spec=pltpu.PrefetchScalarGridSpec(
            num_scalar_prefetch=1,
            grid=(rows // tile,),
            in_specs=[row, row, whole(wu.shape), whole(bu.shape), whole(wd.shape), whole(vec.shape)],
            out_specs=[wide, wide, row, row, row, pl.BlockSpec((8, d), lambda i, c: (0, 0))],
        ),
        out_shape=[
            jax.ShapeDtypeStruct((rows, ff), BF),
            jax.ShapeDtypeStruct((rows, ff), BF),
            jax.ShapeDtypeStruct((rows, d), BF),
            jax.ShapeDtypeStruct((rows, d), F32),
            jax.ShapeDtypeStruct((rows, d), BF),
            jax.ShapeDtypeStruct((8, d), F32),
        ],
        compiler_params=params(),
        name="ffn_forward",
    )(code, n, cot, wu, bu, wd, vec)


def backward_body(gd_ref, gh_ref, g_ref, h_ref, wu_ref, wd_ref, v_ref, gu_ref, g1_ref, ga_ref, s_ref, bu_ref):
    step = pl.program_id(0)

    @pl.when(step == 0)
    def _():
        s_ref[...] = jnp.zeros_like(s_ref)
        bu_ref[...] = jnp.zeros_like(bu_ref)

    d = gd_ref.shape[1]
    gd = gd_ref[...]
    gn = gh_ref[...]
    for j in range(wu_ref.shape[1] // d):
        cols = slice(j * d, (j + 1) * d)
        gu = (mm_nt(gd, wd_ref[cols, :]) * g_ref[:, cols].astype(F32)).astype(BF)
        gu_ref[:, cols] = gu
        bu_ref[0:1, cols] += jnp.sum(gu.astype(F32), 0, keepdims=True)
        gn = gn + mm_nt(gu, wu_ref[:, cols])
    xhat, r = row_norm(h_ref[...])
    g = gn * v_ref[1:2, :]
    gh = r * (g - jnp.mean(g, -1, keepdims=True) - xhat * jnp.mean(g * xhat, -1, keepdims=True))
    g1_ref[...] = gh
    ga = gh.astype(BF)
    ga_ref[...] = ga
    s_ref[0:1, :] += jnp.sum(gn * xhat, 0, keepdims=True)
    s_ref[1:2, :] += jnp.sum(gn, 0, keepdims=True)
    s_ref[2:3, :] += jnp.sum(ga.astype(F32), 0, keepdims=True)


def backward_call(gd, gh, g, h, wu, wd, vec, tile=512):
    rows, d = gd.shape
    ff = wu.shape[1]
    row = pl.BlockSpec((tile, d), lambda i: (i, 0))
    wide = pl.BlockSpec((tile, ff), lambda i: (i, 0))
    return pl.pallas_call(
        backward_body,
        grid=(rows // tile,),
        in_specs=[row, row, wide, row, whole(wu.shape), whole(wd.shape), whole(vec.shape)],
        out_specs=[wide, row, row, pl.BlockSpec((8, d), lambda i: (0, 0)), pl.BlockSpec((8, ff), lambda i: (0, 0))],
        out_shape=[
            jax.ShapeDtypeStruct((rows, ff), BF),
            jax.ShapeDtypeStruct((rows, d), F32),
            jax.ShapeDtypeStruct((rows, d), BF),
            jax.ShapeDtypeStruct((8, d), F32),
            jax.ShapeDtypeStruct((8, ff), F32),
        ],
        compiler_params=params(),
        name="ffn_backward",
    )(gd, gh, g, h, wu, wd, vec)


def attend_back_body(code, ga_ref, q_ref, pk_ref, p_ref, kv_ref, w_ref, proj_ref, pt_ref,
                     gq_ref, gkv_ref, gp_ref, s_ref, low, high, gc):
    step = pl.program_id(0)
    upper = step % 2
    single = code[step // 2] == 0
    half, d = q_ref.shape
    k = pk_ref.shape[1]
    scale = 1.0 / math.sqrt(d // HEADS)

    @pl.when(step == 0)
    def _():
        s_ref[...] = jnp.zeros_like(s_ref)
        gp_ref[...] = jnp.zeros_like(gp_ref)

    gc[...] = mm_nt(ga_ref[...], w_ref[...]).astype(BF)
    left = pair_mask(k)
    for i in range(HEADS // 2):
        cols = slice(128 * i, 128 * (i + 1))
        vcols = slice(d + 128 * i, d + 128 * (i + 1))
        q = q_ref[:, cols] * jnp.asarray(scale, BF)
        g = gc[:, cols]
        kp = pk_ref[0, :, cols] * jnp.asarray(scale, BF)
        vp = pk_ref[0, :, vcols]
        zero = jnp.zeros_like(kp)
        gq = None
        gk = []
        gv = []
        for s in range(2):
            keep = left if s == 0 else jnp.logical_not(left)
            km = jnp.where(keep, kp, zero)
            vm = jnp.where(keep, vp, zero)
            p16 = p_ref[0, 2 * i + s]
            p = p16.astype(F32)
            t = p * mm_nt(vm, g)
            ds = (t - p * jnp.sum(t, 0, keepdims=True)).astype(BF)
            part = mm_tn(ds, km)
            gq = part if gq is None else gq + part
            gk.append(mm(ds, q))
            gv.append(mm(p16, g))
        gq = gq.astype(BF)
        gq_ref[:, cols] = gq
        s_ref[0:1, cols] += jnp.sum(gq.astype(F32), 0, keepdims=True)
        high[:, cols] = jnp.where(left, gk[0], gk[1])
        high[:, vcols] = jnp.where(left, gv[0], gv[1])

    @pl.when(upper == 0)
    def _():
        low[...] = high[...]

    @pl.when(upper == 1)
    def _():
        merged = low[...] + high[...]
        first = jnp.where(single, merged, low[...]).astype(BF)
        second = jnp.where(single, merged, high[...]).astype(BF)
        lower = mm(pt_ref[:half, :], first).astype(BF)
        gkv_ref[:half, :] = lower
        block = jnp.where(single, pt_ref[half:, :], pt_ref[:half, :])
        higher = mm(block, second).astype(BF)
        gkv_ref[half:, :] = higher
        s_ref[0:1, d:] += jnp.sum(lower.astype(F32), 0, keepdims=True) + jnp.sum(higher.astype(F32), 0, keepdims=True)
        one = mm_nt(first, kv_ref[:half, :])
        two = mm_nt(second, kv_ref[half:, :])
        gp_ref[:, :half] += one + jnp.where(single, 0.0, two)
        gp_ref[:, half:] += jnp.where(single, two, 0.0)


def attend_back_call(code, ga, q, pk, p, kv, w, proj):
    n, d = ga.shape
    steps, k, _ = pk.shape
    half = n // steps
    pt = proj.T
    row = pl.BlockSpec((half, d), lambda i, c: (i, 0))
    both = pl.BlockSpec((2 * half, 2 * d), lambda i, c: (i // 2, 0))
    return pl.pallas_call(
        attend_back_body,
        grid_spec=pltpu.PrefetchScalarGridSpec(
            num_scalar_prefetch=1,
            grid=(steps,),
            in_specs=[
                row,
                row,
                pl.BlockSpec((1, k, 2 * d), lambda i, c: (i, 0, 0)),
                pl.BlockSpec((1, HEADS, k, half), lambda i, c: (i, 0, 0, 0)),
                both,
                whole(w.shape),
                whole(proj.shape),
                whole(pt.shape),
            ],
            out_specs=[
                row,
                both,
                pl.BlockSpec((k, 2 * half), lambda i, c: (0, 0)),
                pl.BlockSpec((8, 3 * d), lambda i, c: (0, 0)),
            ],
            scratch_shapes=[pltpu.VMEM((k, 2 * d), F32), pltpu.VMEM((k, 2 * d), F32), pltpu.VMEM((half, d), BF)],
        ),
        out_shape=[
            jax.ShapeDtypeStruct((n, d), BF),
            jax.ShapeDtypeStruct((n, 2 * d), BF),
            jax.ShapeDtypeStruct((k, 2 * half), F32),
            jax.ShapeDtypeStruct((8, 3 * d), F32),
        ],
        compiler_params=params(),
        name="attend_backward",
    )(code, ga, q, pk, p, kv, w, proj, pt)


def token_body(g1_ref, gq_ref, gkv_ref, w_ref, o_ref):
    d = gq_ref.shape[1]
    o_ref[...] = (
        g1_ref[...] + mm_nt(gq_ref[...], w_ref[:, :d]) + mm_nt(gkv_ref[...], w_ref[:, d:])
    ).astype(BF)


def token_call(g1, gq, gkv, w, tile=512):
    n, d = g1.shape
    row = pl.BlockSpec((tile, d), lambda i: (i, 0))
    return pl.pallas_call(
        token_body,
        grid=(n // tile,),
        in_specs=[row, row, pl.BlockSpec((tile, 2 * d), lambda i: (i, 0)), whole(w.shape)],
        out_specs=row,
        out_shape=jax.ShapeDtypeStruct((n, d), BF),
        compiler_params=params(),
        name="token_grad",
    )(g1, gq, gkv, w)


AXES = ("dp", "fsdp")


class Ring:
    def __init__(self, devices):
        self.n = devices
        self.nz = devices // 8
        me = lax.axis_index(AXES)
        self.core = me % 2
        self.x = (me // 2) % 2
        self.y = (me // 4) % 2
        self.z = me // 8

    def move(self, value, target):
        return lax.ppermute(value, AXES, [(i, target(i)) for i in range(self.n)])

    def shift(self, value, k):
        return self.move(value, lambda i: (i + 8 * k) % self.n)

    def first(self, value):
        return self.move(value, lambda i: i ^ (2 if i % 2 == 0 else 4))

    def second(self, value):
        return self.move(value, lambda i: i ^ (4 if i % 2 == 0 else 2))

    def swap(self, value):
        return self.move(value, lambda i: i ^ 1)

    def gather(self, shard):
        own = jnp.stack([shard] + [self.shift(shard, k) for k in range(1, self.nz)])
        own = jnp.concatenate([own, self.first(own)])
        own = jnp.concatenate([own, self.second(own)])
        return jnp.concatenate([own, self.swap(own)])

    def gather_order(self):
        d = jnp.arange(self.n)
        c, x, y, z = d % 2, (d // 2) % 2, (d // 4) % 2, d // 8
        dx, dy, k = x ^ self.x, y ^ self.y, (self.z - z) % self.nz
        near, far = jnp.where(c == 0, dx, dy), jnp.where(c == 0, dy, dx)
        return ((c ^ self.core) * 4 + far * 2 + near) * self.nz + k

    def scatter_order(self, core):
        j = jnp.arange(self.n // 2)
        k, near, far = j % self.nz, (j // self.nz) % 2, j // (2 * self.nz)
        dx, dy = jnp.where(core == 0, near, far), jnp.where(core == 0, far, near)
        return (((self.z + k) % self.nz * 2 + (self.y ^ dy)) * 2 + (self.x ^ dx)) * 2 + core

    def scatter(self, blocks):
        take = lambda order: blocks.at[order].get(mode="promise_in_bounds")
        nz = self.nz
        send, keep = take(self.scatter_order(1 - self.core)), take(self.scatter_order(self.core))
        add = lambda parts: sum(p.astype(F32) for p in parts)
        r0 = self.swap(send)
        r1 = self.second(add([keep[2 * nz :], r0[2 * nz :]]).astype(BF))
        r2 = self.first(add([keep[nz : 2 * nz], r0[nz : 2 * nz], r1[nz:]]).astype(BF))
        parts = [keep, r0, r1, r2]
        last = [self.shift(add([p[k] for p in parts]).astype(BF), k) for k in range(1, nz)]
        return add([p[0] for p in parts] + last)


def column_parts(block, width):
    return [block[..., j : j + width] for j in range(0, block.shape[-1], width)]


def pack_small(line, proj, width):
    pad = [(0, 0)] * (line.ndim - 1)
    rows, room = proj.shape[-2], 2 * width - proj.shape[-1]
    line = jnp.pad(line, pad + [(0, room - line.shape[-1])])
    head = jnp.pad(line[..., None, :], pad + [(0, rows - 1), (0, 0)])
    return [proj[..., :width], jnp.concatenate([head, proj[..., width:]], -1)]


def unpack_small(first, second, length, columns):
    width = first.shape[-1]
    room = 2 * width - columns
    return second[..., 0, :length], jnp.concatenate([first, second[..., room:]], -1)


def split_line(line, sizes):
    parts, at = [], 0
    for size in sizes:
        parts.append(line[:, at : at + size].reshape(-1))
        at += size
    return parts


def stack_rows(*vectors):
    width = vectors[0].shape[0]
    rows = [v.astype(F32).reshape(1, -1) for v in vectors]
    return jnp.concatenate(rows + [jnp.zeros((8 - len(rows), width), F32)], 0)


def local(
    tokens,
    cotangent,
    bucket_code,
    qkv_weight,
    qkv_bias,
    projection,
    out_weight,
    out_bias,
    norm_gain,
    norm_shift,
    up_weight,
    up_bias,
    down_weight,
    down_bias,
    final_gain,
    final_shift,
    *,
    devices,
):
    d = tokens.shape[1]
    ring = Ring(devices)
    small = (qkv_bias, out_bias, norm_gain, norm_shift, up_bias, down_bias, final_gain, final_shift)
    sizes = [v.shape[0] for v in small]
    length = sum(sizes)
    r, rp, rd = qkv_weight.shape[0], projection.shape[0], down_weight.shape[0]
    full = lambda block: block.reshape(-1, block.shape[-1])

    one = jnp.concatenate(
        column_parts(qkv_weight, d) + pack_small(jnp.concatenate(small), projection, d), 0
    )
    two = jnp.concatenate([out_weight] + column_parts(up_weight, d), 0)
    one = ring.gather(one)
    two = ring.gather(two)
    three = ring.gather(down_weight)
    order = ring.gather_order()
    pick = lambda pieces, lo, hi: pieces[:, lo:hi].at[order].get(mode="promise_in_bounds")
    wqkv = jnp.concatenate([full(pick(one, j * r, (j + 1) * r)) for j in range(3)], 1)
    line, proj = unpack_small(
        pick(one, 3 * r, 3 * r + rp), pick(one, 3 * r + rp, 3 * r + 2 * rp), length, projection.shape[1]
    )
    proj = full(proj)
    bqkv, bout, ng, ns, bup, bdown, fg, fs = split_line(line, sizes)
    wout = full(pick(two, 0, r))
    wup = jnp.concatenate([full(pick(two, r * j, r * (j + 1))) for j in range(1, 5)], 1)
    wdown = full(pick(three, 0, rd))

    v1 = stack_rows(bout, ng, ns)
    v2 = stack_rows(bdown, fg, fs)
    flat = lambda v: v.astype(F32).reshape(1, -1)
    q, kv, pk = qkv_call(bucket_code, tokens, wqkv, flat(bqkv), proj)
    p, ctx, h1, normed = attend_call(tokens, q, pk, wout, v1)
    act, slope, out, gh2, gd, s2 = forward_call(
        bucket_code, normed, cotangent, wup, flat(bup), wdown, v2
    )
    blocks = lambda grad: grad.reshape(devices, grad.shape[0] // devices, grad.shape[1])
    dwdown = mm_tn(act, gd).astype(BF)
    down_share = ring.scatter(blocks(dwdown))
    gu, gh1, ga, s1, sbu = backward_call(gd, gh2, slope, h1, wup, wdown, v1)
    dwup = mm_tn(normed, gu).astype(BF)
    dwout = mm_tn(ctx, ga).astype(BF)
    two_share = ring.scatter(
        jnp.concatenate([blocks(dwout)] + column_parts(blocks(dwup), d), 1)
    )
    gq, gkv, gproj, sq = attend_back_call(bucket_code, ga, q, pk, p, kv, wout, proj)
    dwq = mm_tn(tokens, gq).astype(BF)
    dwkv = mm_tn(tokens, gkv).astype(BF)
    vectors = (sq[0], s1[2], s1[0], s1[1], sbu[0], s2[2], s2[0], s2[1])
    grad_line = jnp.concatenate([v.reshape(devices, -1) for v in vectors], 1)
    one_share = ring.scatter(
        jnp.concatenate(
            [blocks(dwq)]
            + column_parts(blocks(dwkv), d)
            + [b.astype(BF) for b in pack_small(grad_line, blocks(gproj), d)],
            1,
        )
    )
    tg = token_call(gh1, gq, gkv, wqkv)

    gline, gproj = unpack_small(
        one_share[3 * r : 3 * r + rp], one_share[3 * r + rp :], length, projection.shape[1]
    )
    gb = split_line(gline[None], sizes)
    gqkv = jnp.concatenate([one_share[j * r : (j + 1) * r] for j in range(3)], 1)
    gup = jnp.concatenate([two_share[j * r : (j + 1) * r] for j in range(1, 5)], 1)
    return (
        out, tg, gqkv, gb[0], gproj, two_share[:r], gb[1], gb[2], gb[3],
        gup, gb[4], down_share, gb[5], gb[6], gb[7],
    )


def solution(mesh):
    devices = mesh.size
    matrix, vector = P(AXES, None), P(AXES)
    return jax.shard_map(
        functools.partial(local, devices=devices),
        mesh=mesh,
        in_specs=(
            matrix, matrix, vector, matrix, vector, matrix, matrix, vector,
            vector, vector, matrix, vector, matrix, vector, vector, vector,
        ),
        out_specs=(
            matrix, matrix, matrix, vector, matrix, matrix, vector, vector,
            vector, matrix, vector, matrix, vector, vector, vector,
        ),
        check_vma=False,
    )
```
